32 devices in a mesh: rep: 8 (over z, x), fsdp: 4 (over y, core).
Axes of the slice: x: 2, y: 2, z: 4, core: 2. Of those that a mesh axis runs over, the one named last changes fastest.
Arguments:
- activations: bfloat16 [8, 512, 8192], P('rep', 'fsdp'), may hold values from -6 to 6
- cotangent: bfloat16 [8, 512, 1024], P('rep', 'fsdp'), may hold values from -0.02734375 to 0.02734375
- momentum: float32 [8, 8192, 1024], P('rep', 'fsdp'), may hold values from -6 to 6
- positions: int32 [8, 2048, 32], P('rep', 'fsdp'), may hold values from 0 to 4095, as said below
Outputs:
- new_momentum: float32 [8, 8192, 1024], P('rep', 'fsdp')
- step: float32 [8192, 1024], P('fsdp')
The draws below stay inside these ranges and needn't reach their ends.
Inputs may be any that keep to these rules, and one draw needn't show every extreme that they name: Within one replica and one group the 32 positions are distinct.
All inputs are finite; a program needn't handle non-finite values.
Results may differ from the reference program's by a relative error of at most 0.0017.
Values may be sent and summed in bfloat16 or wider, within the bound.
No kernel may reach another device: no remote copies, remote signals or barrier semaphores. Data moves between devices by JAX's collectives and lax.ppermute only.
A program may use at most 192 MiB of HBM per device.

```python
import jax
import jax.numpy as jnp
from jax import lax

D = 8192
KVD = 1024
GROUP = 64
TOPK = 32
TOK_DEV = 128
TOK_REP = 512
GROUPS = 2048
N_REP = 8
N_FSDP = 4


def draw_positions(key, part):

    def one_replica(subkey):
        scores = jax.random.randint(subkey, (GROUPS, GROUP * GROUP), 0, 2 ** 18) * (GROUP * GROUP)
        scores = scores + jnp.arange(GROUP * GROUP, dtype=jnp.int32)[None, :]
        return lax.top_k(scores, TOPK)[1].astype(jnp.int32)
    subkeys = jax.random.split(jax.random.fold_in(key, 71), N_REP)
    return lax.map(one_replica, subkeys)


def spiked(entries, stream_key, source, target, shards_of, factor):
    def block_of(position):
        return (jnp.arange(entries.shape[position]) // (entries.shape[position] // shards_of)).reshape((-1,) + (1,) * (entries.ndim - 1 - position))

    near = jax.random.permutation(stream_key, shards_of)[block_of(target)]
    other_side = (block_of(target) + shards_of // 2) % shards_of
    return jnp.where((block_of(source) == near) | (block_of(source) == other_side), factor * entries, entries)


def steps_of(key, shape, shards, least, top_value):
    factor_of, own = 1.0, jax.random.fold_in(key, 6)
    for axis_at, parts in shards:
        draws = jnp.exp(jax.random.uniform(jax.random.fold_in(own, axis_at), (parts,), jnp.float32, least / len(shards), top_value / len(shards)))
        factor_of = factor_of * jnp.repeat(draws, shape[axis_at] // parts).reshape([-1 if axis == axis_at else 1 for axis in range(len(shape))])
    return factor_of


def gaussian(key, shape, deviation, reach, cuts=(), kind=jnp.bfloat16):
    values = deviation * jax.random.normal(key, shape, jnp.float32)
    if cuts:
        values = values * steps_of(key, shape, cuts, -0.22, 0.18)
    return jnp.clip(values, -reach, reach).astype(kind)


def gaussian_with(own_key, dims, deviation, reach, pieces, heavy, held_as=jnp.bfloat16):
    array = deviation * jax.random.normal(own_key, dims, jnp.float32)
    if pieces:
        array = array * steps_of(own_key, dims, pieces, -0.22, 0.18)
    return jnp.clip(spiked(array, jax.random.fold_in(own_key, 3), *heavy), -reach, reach).astype(held_as)


def setup_inputs(seed: int = 0) -> dict:
    splits = jax.random.split(jax.random.key(seed), 5)
    return {
        "activations": gaussian_with(splits[0], (N_REP, TOK_REP, D), 1.0, 6.0, ((0, 8), (1, 4)), (1, 2, 4, 2.0)),
        "cotangent": gaussian(splits[1], (N_REP, TOK_REP, KVD), (100 * TOK_DEV * N_FSDP) ** -0.5, 0.02734375, ((0, 8), (1, 4))),
        "momentum": gaussian(splits[2], (N_REP, D, KVD), 1.0, 6.0, ((0, 8), (1, 4)), jnp.float32),
        "positions": draw_positions(jax.random.fold_in(splits[4], 71), 0),
    }


momentum_decay = 0.999
sharpness = 4.0

def dct_table(extent):
    frequency = jnp.arange(extent, dtype=jnp.float32)[:, None]
    location = jnp.arange(extent, dtype=jnp.float32)[None, :]
    cosines = jnp.cos(jnp.pi * (2.0 * location + 1.0) * frequency / (2.0 * extent)) * jnp.sqrt(2.0 / extent)
    return jnp.where(frequency == 0.0, cosines * jnp.sqrt(0.5), cosines)

def forward_dct(spatial, cosines):
    row_count, col_count = spatial.shape
    extent = cosines.shape[0]
    blocks = spatial.reshape(row_count // extent, extent, col_count // extent, extent)
    coeffs = jnp.einsum('hi,piqj,lj->pqhl', cosines, blocks, cosines, precision=lax.Precision.HIGHEST)
    return coeffs.reshape(-1, extent * extent)

def inverse_dct(coeffs, cosines, row_count, col_count):
    extent = cosines.shape[0]
    grid_form = coeffs.reshape(row_count // extent, col_count // extent, extent, extent)
    spatial = jnp.einsum('hi,pqhl,lj->piqj', cosines, grid_form, cosines, precision=lax.Precision.HIGHEST)
    return spatial.reshape(row_count, col_count)

def scatter_groups(values, spot_list):
    group_count = values.shape[0]
    dense_groups = jnp.zeros((group_count, GROUP * GROUP), jnp.float32)
    group_index = jnp.arange(group_count, dtype=jnp.int32)[:, None]
    return dense_groups.at[group_index, spot_list].add(values)

def reference(activations, cotangent, momentum, positions):
    cosines = dct_table(GROUP)

    def replica_step(summed, inputs):
        tokens, upstream, moment, spot_list = inputs
        tokens = tokens.reshape(N_FSDP, TOK_DEV, D)
        upstream = upstream.reshape(N_FSDP, TOK_DEV, KVD)

        def add_block(running, pair):
            product = lax.dot_general(pair[0], pair[1], (((0,), (0,)), ((), ())), preferred_element_type=jnp.float32)
            rounded = lax.optimization_barrier(product.astype(jnp.bfloat16))
            return (running + rounded.astype(jnp.float32), None)
        gradient, _ = lax.scan(add_block, jnp.zeros((D, KVD), jnp.float32), (tokens, upstream))
        updated = momentum_decay * moment + gradient
        coeffs = forward_dct(updated, cosines)
        values = jnp.take_along_axis(coeffs, spot_list, axis=1)
        own_groups = scatter_groups(values, spot_list)
        next_moment = updated - inverse_dct(own_groups, cosines, D, KVD)
        return (summed + own_groups, next_moment)
    summed, new_momentum = lax.scan(replica_step, jnp.zeros((GROUPS, GROUP * GROUP), jnp.float32), (activations, cotangent, momentum, positions))
    update = inverse_dct(summed, cosines, D, KVD)
    return (new_momentum, jnp.tanh(sharpness * update))
```

```python
import functools

import jax
import jax.numpy as jnp
import numpy as np
from jax import lax
from jax.experimental import pallas as pl
from jax.experimental.pallas import tpu as pltpu
from jax.sharding import PartitionSpec as P

GROUP = 64
LANES = 128
WIDE = 256
CHUNKS = 2


momentum_decay = 0.999
sharpness = 4.0


def dct_table(extent):
    frequency = np.arange(extent, dtype=np.float64)[:, None]
    location = np.arange(extent, dtype=np.float64)[None, :]
    cosines = np.cos(np.pi * (2.0 * location + 1.0) * frequency / (2.0 * extent))
    cosines = cosines * np.sqrt(2.0 / extent)
    cosines[0] *= np.sqrt(0.5)
    return cosines.astype(np.float32)


def bf16_parts(x):
    high = x.astype(jnp.bfloat16)
    return high, (x - high.astype(np.float32)).astype(jnp.bfloat16)


def forward_matrix(cosines):
    high, low = bf16_parts(np.kron(np.eye(WIDE // GROUP, dtype=np.float32), cosines.T))
    return np.concatenate([high, high, low], axis=0)


def side_matrix(cosines):
    high, low = bf16_parts(cosines.T)
    return np.concatenate([high, high, low, low], axis=1)


def right_matrix(cosines):
    high, low = bf16_parts(np.kron(np.eye(LANES // GROUP, dtype=np.float32), cosines))
    upper = np.concatenate([high, low], axis=1)
    return np.concatenate([upper, np.concatenate([high, np.zeros_like(low)], axis=1)], axis=0)


def all_matrices(cosines):
    parts = [forward_matrix(cosines), right_matrix(cosines), side_matrix(cosines)]
    return np.concatenate(parts, axis=0)


FORWARD = slice(0, 3 * WIDE)
RIGHT = slice(3 * WIDE, 4 * WIDE)
SIDE = slice(4 * WIDE, 4 * WIDE + GROUP)


def halves(x):
    high = x.astype(jnp.bfloat16)
    return high, (x - high.astype(jnp.float32)).astype(jnp.bfloat16)


def nt_dot(a, b):
    return lax.dot_general(a, b, (((1,), (1,)), ((), ())), preferred_element_type=jnp.float32)


def right_product(x, stacked):
    high, low = halves(x)
    return jnp.dot(
        jnp.concatenate([high, low, high], axis=1), stacked, preferred_element_type=jnp.float32
    )


def local_kernel(sources, kept, *refs):
    token_refs, upstream_refs = refs[:sources], refs[sources : 2 * sources]
    moment_ref, spot_ref, matrix_ref = refs[2 * sources : 2 * sources + 3]
    next_ref, value_ref, half_ref = refs[-3:]
    rows, cols = moment_ref.shape
    per_row = LANES // kept
    lane = lax.broadcasted_iota(jnp.int32, (8, LANES), 1)
    first = lane < 2 * kept
    shift = GROUP * ((lane // kept) % 2)
    side = matrix_ref[SIDE, :].astype(jnp.float32)
    side = side[:, :LANES] + side[:, LANES:]
    table = [side[8 * k : 8 * k + 8, :] for k in range(GROUP // 8)]
    lane_group = lax.broadcasted_iota(jnp.int32, (WIDE, LANES), 1) // kept
    row_group = lax.broadcasted_iota(jnp.int32, (WIDE, LANES), 0) // GROUP
    diagonal = lane_group == row_group
    zero = jnp.zeros((), jnp.bfloat16)
    gradient = lax.dot_general(
        jnp.concatenate([r[...] for r in token_refs], axis=0),
        jnp.concatenate([r[...] for r in upstream_refs], axis=0),
        (((0,), (0,)), ((), ())),
        preferred_element_type=jnp.float32,
    )
    next_ref[...] = momentum_decay * moment_ref[...] + gradient
    for c in range(cols // WIDE):
        span = slice(c * WIDE, c * WIDE + WIDE)
        half_ref[:, span] = right_product(next_ref[:, span], matrix_ref[FORWARD, :])
    for p in range(rows // GROUP):
        for c in range(cols // WIDE):
            at = p * (cols // WIDE) + c
            spots = jnp.broadcast_to(spot_ref[0, at : at + 1, :], (8, LANES))
            upper, lower = spots // GROUP, spots % GROUP
            where = lower + shift
            total = jnp.zeros((8, LANES), jnp.float32)
            upper_rows, lower_rows = [], []
            for k in range(GROUP // 8):
                block = slice(p * GROUP + 8 * k, p * GROUP + 8 * k + 8)
                low_half = half_ref[block, c * WIDE : c * WIDE + LANES]
                high_half = half_ref[block, c * WIDE + LANES : c * WIDE + WIDE]
                one = jnp.take_along_axis(low_half, where, axis=1)
                two = jnp.take_along_axis(high_half, where, axis=1)
                up = jnp.take_along_axis(table[k], upper, axis=1)
                total = total + jnp.where(first, one, two) * up
                upper_rows.append(up)
                lower_rows.append(jnp.take_along_axis(table[k], lower, axis=1))
            value = jnp.sum(total, axis=0, keepdims=True)
            value_ref[0, at : at + 1, :] = value
            s_high, s_low = halves(jnp.concatenate(upper_rows, axis=0) * value)
            b_high, b_low = halves(jnp.concatenate(lower_rows, axis=0))
            r_high = jnp.where(diagonal, jnp.concatenate([b_high] * per_row, axis=0), zero)
            r_low = jnp.where(diagonal, jnp.concatenate([b_low] * per_row, axis=0), zero)
            own = nt_dot(
                jnp.concatenate([s_high, s_low, s_high], axis=1),
                jnp.concatenate([r_high, r_high, r_low], axis=1),
            )
            block, span = slice(p * GROUP, p * GROUP + GROUP), slice(c * WIDE, c * WIDE + WIDE)
            next_ref[block, span] = next_ref[block, span] - own


def shared_kernel(kept, replicas, *refs):
    value_refs, spot_refs = refs[:replicas], refs[replicas : 2 * replicas]
    matrix_ref = refs[2 * replicas]
    step_ref, dense_ref = refs[-2:]
    values = [r[0] for r in value_refs]
    spots = [r[0] for r in spot_refs]
    depth = len(values) * kept
    rows, cols = step_ref.shape
    per_row = LANES // kept
    level = lax.broadcasted_iota(jnp.int32, (GROUP, depth), 0)
    level = level.astype(jnp.float32).astype(jnp.bfloat16)
    zero = jnp.zeros((), jnp.bfloat16)
    one = jnp.ones((), jnp.bfloat16)

    def filled(x, at):
        tile = jnp.broadcast_to(x[at : at + 1], (16, depth)).astype(jnp.bfloat16)
        return jnp.concatenate([tile] * (GROUP // 16), axis=0)

    for a in range(per_row):
        span = slice(a * kept, a * kept + kept)
        group_values = jnp.concatenate([v[:, span] for v in values], axis=1)
        group_spots = jnp.concatenate([s[:, span] for s in spots], axis=1)
        high, low = halves(group_values)
        high, low = high.astype(jnp.float32), low.astype(jnp.float32)
        upper = (group_spots // GROUP).astype(jnp.float32)
        lower = (group_spots % GROUP).astype(jnp.float32)
        for at in range(group_values.shape[0]):
            p, c = at // (cols // WIDE), at % (cols // WIDE)
            hot_upper = jnp.where(level == filled(upper, at), one, zero)
            match = level == filled(lower, at)
            hot_high = jnp.where(match, filled(high, at), zero)
            hot_low = jnp.where(match, filled(low, at), zero)
            dense = nt_dot(hot_upper, hot_high) + nt_dot(hot_upper, hot_low)
            place = slice(c * WIDE + a * GROUP, c * WIDE + a * GROUP + GROUP)
            dense_ref[p * GROUP : p * GROUP + GROUP, place] = dense
    pieces = []
    for c in range(cols // WIDE):
        parts = []
        for p in range(rows // GROUP):
            tile = dense_ref[p * GROUP : p * GROUP + GROUP, c * WIDE : c * WIDE + WIDE]
            high, low = halves(tile)
            stack = jnp.concatenate([high, low, high], axis=0)
            parts.append(jnp.dot(matrix_ref[SIDE, : 3 * GROUP], stack, preferred_element_type=jnp.float32))
        high, low = halves(jnp.concatenate(parts, axis=0))
        for b in range(WIDE // LANES):
            span = slice(b * LANES, b * LANES + LANES)
            pieces.append(jnp.concatenate([high[:, span], low[:, span]], axis=1))
    product = jnp.dot(
        jnp.concatenate(pieces, axis=0), matrix_ref[RIGHT, :], preferred_element_type=jnp.float32
    )
    for b in range(len(pieces)):
        part = product[b * rows : b * rows + rows]
        update = part[:, :LANES] + part[:, LANES:]
        step_ref[:, b * LANES : b * LANES + LANES] = jnp.tanh(sharpness * update)


def swap(x, axis, count, offset):
    return lax.ppermute(x, axis, [(i, i ^ offset) for i in range(count)])


def spread(x, count):
    even = [x]
    even += [swap(x, "rep", count, offset) for offset in range(2, count, 2)]
    odd = [swap(part, "rep", count, 1) for part in even]
    return even + odd


def local_call(sources, kept, blocks, at, columns, incoming, moment, spots, consts, previous):
    row_count, col_count = moment.shape
    tok = columns[0].shape[0]
    spot_rows = spots.shape[1]
    whole = pl.BlockSpec(memory_space=pltpu.VMEM)
    aliased = [] if previous is None else [previous]
    rows = blocks * WIDE
    return pl.pallas_call(
        functools.partial(local_kernel, sources, kept),
        grid=(blocks,),
        in_specs=[pl.BlockSpec((tok, WIDE), lambda i: (0, i))] * sources
        + [whole] * sources
        + [
            pl.BlockSpec((WIDE, col_count), lambda i: (at + i, 0)),
            pl.BlockSpec((1, spot_rows, LANES), lambda i: (at + i, 0, 0)),
        ]
        + [whole] * len(consts)
        + [pl.BlockSpec(memory_space=pl.ANY)] * len(aliased),
        out_specs=[
            pl.BlockSpec((WIDE, col_count), lambda i: (at + i, 0)),
            pl.BlockSpec((1, spot_rows, LANES), lambda i: (i, 0, 0)),
        ],
        out_shape=[
            jax.ShapeDtypeStruct((row_count, col_count), jnp.float32),
            jax.ShapeDtypeStruct((blocks, spot_rows, LANES), jnp.float32),
        ],
        input_output_aliases={2 * sources + 2 + len(consts): 0} if aliased else {},
        scratch_shapes=[pltpu.VMEM((WIDE, col_count), jnp.float32)],
        compiler_params=pltpu.CompilerParams(vmem_limit_bytes=48 * 2**20),
        cost_estimate=pl.CostEstimate(
            flops=12 * rows * col_count * WIDE, bytes_accessed=8 * rows * col_count, transcendentals=0
        ),
        name="local",
    )(*columns, *incoming, moment, spots, *consts, *aliased)


def shared_call(kept, blocks, at, shape, values, spots, consts, previous):
    _, col_count = shape
    spot_rows = values[0].shape[1]
    whole = pl.BlockSpec(memory_space=pltpu.VMEM)
    replicas = len(values)
    aliased = [] if previous is None else [previous]
    rows = blocks * WIDE
    return pl.pallas_call(
        functools.partial(shared_kernel, kept, replicas),
        grid=(blocks,),
        in_specs=[pl.BlockSpec((1, spot_rows, LANES), lambda i: (i, 0, 0))] * replicas
        + [pl.BlockSpec((1, spot_rows, LANES), lambda i: (at + i, 0, 0))] * replicas
        + [whole] * len(consts)
        + [pl.BlockSpec(memory_space=pl.ANY)] * len(aliased),
        out_specs=pl.BlockSpec((WIDE, col_count), lambda i: (at + i, 0)),
        out_shape=jax.ShapeDtypeStruct(shape, jnp.float32),
        input_output_aliases={2 * replicas + len(consts): 0} if aliased else {},
        scratch_shapes=[pltpu.VMEM((WIDE, col_count), jnp.float32)],
        compiler_params=pltpu.CompilerParams(vmem_limit_bytes=48 * 2**20),
        cost_estimate=pl.CostEstimate(
            flops=12 * rows * col_count * WIDE, bytes_accessed=4 * rows * col_count, transcendentals=0
        ),
        name="shared",
    )(*values, *spots, *consts, *aliased)


def per_device(n_fsdp, n_rep, activations, cotangent, momentum, positions):
    tokens, upstream, moment = activations[0], cotangent[0], momentum[0]
    row_count, col_count = moment.shape
    kept = positions.shape[2]
    steps = row_count // WIDE
    chunks = min(CHUNKS, steps)
    blocks = steps // chunks
    spot_rows = WIDE * col_count // (GROUP * GROUP) * kept // LANES
    me = lax.axis_index("fsdp")
    half = n_fsdp // 2

    def pieces_of(k, me):
        return [
            lax.dynamic_slice_in_dim(
                tokens, (me ^ offset) * row_count + k * blocks * WIDE, blocks * WIDE, 1
            )
            for offset in range(n_fsdp)
        ]

    def exchange(pieces):
        out = [pieces[0]]
        for offset in range(1, n_fsdp):
            out.append(swap(pieces[offset], "fsdp", n_fsdp, offset))
        return out

    incoming = {0: upstream}
    offset = half
    while offset:
        for known in list(incoming):
            incoming[known ^ offset] = swap(incoming[known], "fsdp", n_fsdp, offset)
        offset //= 2
    pieces = pieces_of(0, me)
    me, positions, pieces = lax.optimization_barrier((me, positions, pieces))
    all_columns = [exchange(pieces)]
    for k in range(1, chunks):
        pieces = pieces_of(k, me)
        all_columns.append(exchange(pieces))
    spots = positions[0].reshape(steps, spot_rows, LANES)

    def settled(x):
        return jnp.where(me >= 0, x, jnp.zeros((), x.dtype))

    incoming = [settled(upstream)] + [incoming[i] for i in range(1, n_fsdp)]
    all_spots = spread(spots, n_rep)

    cosines = dct_table(GROUP)
    matrices = (settled(all_matrices(cosines)),)

    next_moment, step, gathered = None, None, []
    for k in range(chunks):
        next_moment, values = local_call(
            n_fsdp, kept, blocks, k * blocks, all_columns[k], incoming, moment, spots,
            matrices, next_moment,
        )
        gathered.append(spread(values, n_rep))
    for k in range(chunks):
        step = shared_call(
            kept, blocks, k * blocks, moment.shape, gathered[k], all_spots, matrices, step
        )
    return (next_moment[None], step)


def solution(mesh):
    spec = P("rep", "fsdp", None)
    return jax.shard_map(
        functools.partial(per_device, mesh.shape["fsdp"], mesh.shape["rep"]),
        mesh=mesh,
        in_specs=(spec, spec, spec, spec),
        out_specs=(spec, P("fsdp", None)),
        check_vma=False,
    )
```

```python
import functools

import jax
import jax.numpy as jnp
import numpy as np
from jax import lax
from jax.experimental import pallas as pl
from jax.experimental.pallas import tpu as pltpu
from jax.sharding import PartitionSpec as P

GROUP = 64
LANES = 128
WIDE = 256


FACTORS = tuple(1.0 + k / 128.0 for k in (1, 2, 10, 15, 24, 25, 28, 61, 74, 82, 94, 97, 98, 107, 113))
PARTS = 2

momentum_decay = 0.999
sharpness = 4.0


def dct_table(extent):
    frequency = np.arange(extent, dtype=np.float64)[:, None]
    location = np.arange(extent, dtype=np.float64)[None, :]
    cosines = np.cos(np.pi * (2.0 * location + 1.0) * frequency / (2.0 * extent))
    cosines = cosines * np.sqrt(2.0 / extent)
    cosines[0] *= np.sqrt(0.5)
    return cosines.astype(np.float32)


def bf16_parts(x):
    high = x.astype(jnp.bfloat16)
    return high, (x - high.astype(np.float32)).astype(jnp.bfloat16)


def forward_matrix(cosines):
    high, low = bf16_parts(np.kron(np.eye(WIDE // GROUP, dtype=np.float32), cosines.T))
    return np.concatenate([high, high, low], axis=0)


def side_matrix(cosines):
    high, low = bf16_parts(cosines.T)
    return np.concatenate([high, high, low, low], axis=1)


def right_matrix(cosines):
    high, low = bf16_parts(np.kron(np.eye(LANES // GROUP, dtype=np.float32), cosines))
    upper = np.concatenate([high, low], axis=1)
    return np.concatenate([upper, np.concatenate([high, np.zeros_like(low)], axis=1)], axis=0)


def all_matrices(cosines):
    parts = [forward_matrix(cosines), right_matrix(cosines), side_matrix(cosines)]
    return np.concatenate(parts, axis=0)


FORWARD = slice(0, 3 * WIDE)
RIGHT = slice(3 * WIDE, 4 * WIDE)
SIDE = slice(4 * WIDE, 4 * WIDE + GROUP)


def halves(x):
    high = x.astype(jnp.bfloat16)
    return high, (x - high.astype(jnp.float32)).astype(jnp.bfloat16)


def nt_dot(a, b):
    return lax.dot_general(a, b, (((1,), (1,)), ((), ())), preferred_element_type=jnp.float32)


def right_product(x, stacked):
    high, low = halves(x)
    return jnp.dot(
        jnp.concatenate([high, low, high], axis=1), stacked, preferred_element_type=jnp.float32
    )


def local_kernel(sources, kept, *refs):
    token_refs, upstream_refs = refs[:sources], refs[sources : 2 * sources]
    moment_ref, spot_ref, matrix_ref = refs[2 * sources : 2 * sources + 3]
    next_ref, message_ref, half_ref, scaled_ref, base_ref, value_ref = refs[-6:]
    rows, cols = moment_ref.shape
    per_row = LANES // kept
    lane = lax.broadcasted_iota(jnp.int32, (8, LANES), 1)
    first = lane < 2 * kept
    shift = GROUP * ((lane // kept) % 2)
    side = matrix_ref[SIDE, :].astype(jnp.float32)
    side = side[:, :LANES] + side[:, LANES:]
    table = [side[8 * k : 8 * k + 8, :] for k in range(GROUP // 8)]
    lane_group = lax.broadcasted_iota(jnp.int32, (WIDE, LANES), 1) // kept
    row_group = lax.broadcasted_iota(jnp.int32, (WIDE, LANES), 0) // GROUP
    lane_wide = lax.broadcasted_iota(jnp.int32, (GROUP, 2 * LANES), 1) % LANES // kept
    zero = jnp.zeros((), jnp.bfloat16)
    gradient = lax.dot_general(
        jnp.concatenate([r[...] for r in token_refs], axis=0),
        jnp.concatenate([r[...] for r in upstream_refs], axis=0),
        (((0,), (0,)), ((), ())),
        preferred_element_type=jnp.float32,
    )
    next_ref[...] = momentum_decay * moment_ref[...] + gradient
    for c in range(cols // WIDE):
        span = slice(c * WIDE, c * WIDE + WIDE)
        half_ref[:, span] = right_product(next_ref[:, span], matrix_ref[FORWARD, :])
    for p in range(rows // GROUP):
        for c in range(cols // WIDE):
            at = p * (cols // WIDE) + c
            spots = jnp.broadcast_to(spot_ref[0, at : at + 1, :], (8, LANES))
            upper, lower = spots // GROUP, spots % GROUP
            where = lower + shift
            total = jnp.zeros((8, LANES), jnp.float32)
            starts = [p * GROUP + 8 * k for k in range(GROUP // 8)]
            low_span = slice(c * WIDE, c * WIDE + LANES)
            high_span = slice(c * WIDE + LANES, c * WIDE + WIDE)
            ones = [jnp.take_along_axis(half_ref[b : b + 8, low_span], where, axis=1) for b in starts]
            twos = [jnp.take_along_axis(half_ref[b : b + 8, high_span], where, axis=1) for b in starts]
            upper_rows = [jnp.take_along_axis(t, upper, axis=1) for t in table]
            lower_rows = [jnp.take_along_axis(t, lower, axis=1) for t in table]
            for one, two, up in zip(ones, twos, upper_rows):
                total = total + jnp.where(first, one, two) * up
            value = jnp.sum(total, axis=0, keepdims=True)
            value_ref[at : at + 1, :] = value
            s_high, s_low = halves(jnp.concatenate(upper_rows, axis=0) * value)
            b_high, b_low = halves(jnp.concatenate(lower_rows, axis=0))
            scaled_ref[at] = jnp.concatenate([s_high, s_low], axis=1)
            base_ref[at] = jnp.concatenate([b_high, b_low], axis=1)
    for p in range(rows // GROUP):
        for c in range(cols // WIDE):
            at = p * (cols // WIDE) + c
            scaled, base = scaled_ref[at], base_ref[at]
            b_high, b_low = base[:, :LANES], base[:, LANES:]
            b_high = jnp.concatenate([b_high, b_high], axis=1)
            b_low = jnp.concatenate([b_low, b_low], axis=1)
            masked = [jnp.where(lane_wide == a, scaled, zero) for a in range(per_row)]
            prod = nt_dot(
                jnp.concatenate(masked, axis=0),
                jnp.concatenate([b_high, b_high, b_low, b_low], axis=0),
            )
            prod = prod[:, :LANES] + prod[:, LANES:]
            left = lax.broadcasted_iota(jnp.int32, (GROUP, LANES), 1) < GROUP
            own = jnp.concatenate([jnp.where(left, prod[2 * b * GROUP : 2 * b * GROUP + GROUP], prod[2 * b * GROUP + GROUP : 2 * b * GROUP + 2 * GROUP]) for b in range(per_row // 2)], axis=1)
            block, span = slice(p * GROUP, p * GROUP + GROUP), slice(c * WIDE, c * WIDE + WIDE)
            next_ref[block, span] = next_ref[block, span] - own
    for n, part in enumerate(as_product(value_ref[...])):
        part = part.astype(jnp.bfloat16)
        for j in range(message_ref.shape[0]):
            message_ref[j, 0, n] = part


def as_product(value):
    best = value.astype(jnp.bfloat16).astype(jnp.float32)
    factor = jnp.ones_like(value)
    error = jnp.abs(best - value)
    for b in FACTORS:
        a = (value * (1.0 / b)).astype(jnp.bfloat16).astype(jnp.float32)
        trial = jnp.abs(a * b - value)
        better = trial < error
        error = jnp.where(better, trial, error)
        best = jnp.where(better, a, best)
        factor = jnp.where(better, b, factor)
    return best, factor


def shared_kernel(kept, *refs):
    message_ref, spot_ref, matrix_ref = refs[:3]
    step_ref, dense_ref = refs[-2:]
    replicas = message_ref.shape[0]
    depth = replicas * kept
    rows, cols = step_ref.shape
    per_row = LANES // kept
    level = lax.broadcasted_iota(jnp.int32, (GROUP, depth), 0)
    level = level.astype(jnp.float32).astype(jnp.bfloat16)
    zero = jnp.zeros((), jnp.bfloat16)

    def filled(x, at):
        tile = jnp.broadcast_to(x[at : at + 1], (16, depth)).astype(jnp.bfloat16)
        return jnp.concatenate([tile] * (GROUP // 16), axis=0)

    parts = [
        [message_ref[j, 0, n].astype(jnp.float32) for j in range(replicas)] for n in range(PARTS)
    ]
    parts.append([spot_ref[j, 0].astype(jnp.int32) for j in range(replicas)])
    for a in range(per_row):
        span = slice(a * kept, a * kept + kept)
        best, factor, place = [jnp.concatenate([x[:, span] for x in p], axis=1) for p in parts]
        upper = (place // GROUP).astype(jnp.float32)
        lower = (place % GROUP).astype(jnp.float32)
        for at in range(best.shape[0]):
            p, c = at // (cols // WIDE), at % (cols // WIDE)
            hot_upper = jnp.where(level == filled(upper, at), filled(factor, at), zero)
            hot_lower = jnp.where(level == filled(lower, at), filled(best, at), zero)
            place = slice(c * WIDE + a * GROUP, c * WIDE + a * GROUP + GROUP)
            dense_ref[p * GROUP : p * GROUP + GROUP, place] = nt_dot(hot_upper, hot_lower)
    pieces = []
    for c in range(cols // WIDE):
        parts = []
        for p in range(rows // GROUP):
            tile = dense_ref[p * GROUP : p * GROUP + GROUP, c * WIDE : c * WIDE + WIDE]
            high, low = halves(tile)
            stack = jnp.concatenate([high, low, high], axis=0)
            parts.append(jnp.dot(matrix_ref[SIDE, : 3 * GROUP], stack, preferred_element_type=jnp.float32))
        high, low = halves(jnp.concatenate(parts, axis=0))
        for b in range(WIDE // LANES):
            span = slice(b * LANES, b * LANES + LANES)
            pieces.append(jnp.concatenate([high[:, span], low[:, span]], axis=1))
    product = jnp.dot(
        jnp.concatenate(pieces, axis=0), matrix_ref[RIGHT, :], preferred_element_type=jnp.float32
    )
    for b in range(len(pieces)):
        part = product[b * rows : b * rows + rows]
        update = part[:, :LANES] + part[:, LANES:]
        step_ref[:, b * LANES : b * LANES + LANES] = jnp.tanh(sharpness * update)


def swap(x, axis, count, offset):
    return lax.ppermute(x, axis, [(i, i ^ offset) for i in range(count)])


def local_call(
    sources, kept, blocks, at, slot, columns, incoming, moment, spots, matrices, next_moment, message
):
    _, col_count = moment.shape
    tok = columns[0].shape[0]
    spot_rows = spots.shape[1]
    whole = pl.BlockSpec(memory_space=pltpu.VMEM)
    aliased, aliases = [], {}
    for position, array in enumerate((next_moment, message)):
        if not isinstance(array, jax.ShapeDtypeStruct):
            aliases[2 * sources + 3 + len(aliased)] = position
            aliased.append(array)
    rows = blocks * WIDE
    return pl.pallas_call(
        functools.partial(local_kernel, sources, kept),
        grid=(blocks,),
        in_specs=[pl.BlockSpec((tok, WIDE), lambda i: (0, i))] * sources
        + [whole] * sources
        + [
            pl.BlockSpec((WIDE, col_count), lambda i: (at + i, 0)),
            pl.BlockSpec((1, spot_rows, LANES), lambda i: (at + i, 0, 0)),
            whole,
        ]
        + [pl.BlockSpec(memory_space=pl.ANY)] * len(aliased),
        out_specs=[
            pl.BlockSpec((WIDE, col_count), lambda i: (at + i, 0)),
            pl.BlockSpec(
                (message.shape[0], 1) + message.shape[2:], lambda i: (0, slot + i, 0, 0, 0)
            ),
        ],
        out_shape=[jax.ShapeDtypeStruct(x.shape, x.dtype) for x in (next_moment, message)],
        input_output_aliases=aliases,
        scratch_shapes=[pltpu.VMEM((WIDE, col_count), jnp.float32)]
        + [pltpu.VMEM((spot_rows, GROUP, 2 * LANES), jnp.bfloat16)] * 2
        + [pltpu.VMEM((spot_rows, LANES), jnp.float32)],
        compiler_params=pltpu.CompilerParams(vmem_limit_bytes=48 * 2**20),
        cost_estimate=pl.CostEstimate(
            flops=12 * rows * col_count * WIDE, bytes_accessed=8 * rows * col_count, transcendentals=0
        ),
        name="local",
    )(*columns, *incoming, moment, spots, matrices, *aliased)


def shared_call(kept, blocks, at, shape, message, spots, matrices, previous):
    col_count = shape[1]
    whole = pl.BlockSpec(memory_space=pltpu.VMEM)
    aliased = [] if previous is None else [previous]
    rows = blocks * WIDE
    return pl.pallas_call(
        functools.partial(shared_kernel, kept),
        grid=(blocks,),
        in_specs=[
            pl.BlockSpec((message.shape[0], 1) + message.shape[2:], lambda i: (0, i, 0, 0, 0)),
            pl.BlockSpec((spots.shape[0], 1) + spots.shape[2:], lambda i: (0, at + i, 0, 0)),
            whole,
        ]
        + [pl.BlockSpec(memory_space=pl.ANY)] * len(aliased),
        out_specs=pl.BlockSpec((WIDE, col_count), lambda i: (at + i, 0)),
        out_shape=jax.ShapeDtypeStruct(shape, jnp.float32),
        input_output_aliases={3: 0} if aliased else {},
        scratch_shapes=[pltpu.VMEM((WIDE, col_count), jnp.float32)],
        compiler_params=pltpu.CompilerParams(vmem_limit_bytes=48 * 2**20),
        cost_estimate=pl.CostEstimate(
            flops=12 * rows * col_count * WIDE, bytes_accessed=4 * rows * col_count, transcendentals=0
        ),
        name="shared",
    )(message, spots, matrices, *aliased)


def chunk_sizes(steps):
    if steps < 4:
        return [1] * steps, [[k] for k in range(steps)]
    first = steps // 2
    return [first, steps - first], [[0], [1]]
    first = steps // 4
    second = (steps - first) // 2
    return [first, second, steps - first - second], [[0, 1], [2]]


def per_device(n_fsdp, n_rep, activations, cotangent, momentum, positions):
    tokens, upstream, moment = activations[0], cotangent[0], momentum[0]
    row_count, col_count = moment.shape
    kept = positions.shape[2]
    steps = row_count // WIDE
    sizes, travel = chunk_sizes(steps)
    starts = [sum(sizes[:k]) for k in range(len(sizes))]
    chunks = len(sizes)
    spot_rows = WIDE * col_count // (GROUP * GROUP) * kept // LANES
    me = lax.axis_index("fsdp")
    half = n_fsdp // 2

    def pieces_of(k, me):
        return [
            lax.dynamic_slice_in_dim(
                tokens, (me ^ offset) * row_count + starts[k] * WIDE, sizes[k] * WIDE, 1
            )
            for offset in range(n_fsdp)
        ]

    def exchange(pieces):
        out = [pieces[0]]
        for offset in range(1, n_fsdp):
            out.append(swap(pieces[offset], "fsdp", n_fsdp, offset))
        return out

    incoming = {0: upstream}
    offset = half
    while offset:
        for known in list(incoming):
            incoming[known ^ offset] = swap(incoming[known], "fsdp", n_fsdp, offset)
        offset //= 2
    pieces = pieces_of(0, me)
    me, positions, pieces = lax.optimization_barrier((me, positions, pieces))
    all_columns = [exchange(pieces)]
    for k in range(1, chunks):
        pieces = pieces_of(k, me)
        all_columns.append(exchange(pieces))
    spots = positions[0].reshape(steps, spot_rows, LANES)

    def settled(x):
        return jnp.where(me >= 0, x, jnp.zeros((), x.dtype))

    incoming = [settled(upstream)] + [incoming[i] for i in range(1, n_fsdp)]

    cosines = dct_table(GROUP)
    matrices = settled(all_matrices(cosines))

    copies = jnp.broadcast_to(spots.astype(jnp.int16)[None], (n_rep,) + spots.shape)
    all_spots = lax.all_to_all(copies, "rep", split_axis=0, concat_axis=0, tiled=True)
    next_moment = jax.ShapeDtypeStruct((row_count, col_count), jnp.float32)
    step, gathered = None, []
    for members in travel:
        blocks = sum(sizes[k] for k in members)
        message = jax.ShapeDtypeStruct((n_rep, blocks, PARTS, spot_rows, LANES), jnp.bfloat16)
        for k in members:
            next_moment, message = local_call(
                n_fsdp, kept, sizes[k], starts[k], starts[k] - starts[members[0]],
                all_columns[k], incoming, moment, spots, matrices, next_moment, message,
            )
        gathered.append(
            lax.all_to_all(message, "rep", split_axis=0, concat_axis=0, tiled=True)
        )
    for g, members in enumerate(travel):
        step = shared_call(
            kept, gathered[g].shape[1], starts[members[0]], moment.shape, gathered[g], all_spots,
            matrices, step,
        )
    return (next_moment[None], step)


def solution(mesh):
    spec = P("rep", "fsdp", None)
    return jax.shard_map(
        functools.partial(per_device, mesh.shape["fsdp"], mesh.shape["rep"]),
        mesh=mesh,
        in_specs=(spec, spec, spec, spec),
        out_specs=(spec, P("fsdp", None)),
        check_vma=False,
    )
```

```python
import functools

import jax
import jax.numpy as jnp
import numpy as np
from jax import lax
from jax.experimental import pallas as pl
from jax.experimental.pallas import tpu as pltpu
from jax.sharding import PartitionSpec as P

GROUP = 64
LANES = 128
WIDE = 256


FACTORS = tuple(1.0 + k / 128.0 for k in (1, 2, 10, 15, 24, 25, 28, 61, 74, 82, 94, 97, 98, 107, 113))
PARTS = 2

momentum_decay = 0.999
sharpness = 4.0


def dct_table(extent):
    frequency = np.arange(extent, dtype=np.float64)[:, None]
    location = np.arange(extent, dtype=np.float64)[None, :]
    cosines = np.cos(np.pi * (2.0 * location + 1.0) * frequency / (2.0 * extent))
    cosines = cosines * np.sqrt(2.0 / extent)
    cosines[0] *= np.sqrt(0.5)
    return cosines.astype(np.float32)


def bf16_parts(x):
    high = x.astype(jnp.bfloat16)
    return high, (x - high.astype(np.float32)).astype(jnp.bfloat16)


def forward_matrix(cosines):
    high, low = bf16_parts(np.kron(np.eye(WIDE // GROUP, dtype=np.float32), cosines.T))
    return np.concatenate([high, high, low], axis=0)


def side_matrix(cosines):
    high, low = bf16_parts(cosines.T)
    return np.concatenate([high, high, low, low], axis=1)


def right_matrix(cosines):
    high, low = bf16_parts(np.kron(np.eye(LANES // GROUP, dtype=np.float32), cosines))
    upper = np.concatenate([high, low], axis=1)
    return np.concatenate([upper, np.concatenate([high, np.zeros_like(low)], axis=1)], axis=0)


def all_matrices(cosines):
    parts = [forward_matrix(cosines), right_matrix(cosines), side_matrix(cosines)]
    return np.concatenate(parts, axis=0)


FORWARD = slice(0, 3 * WIDE)
RIGHT = slice(3 * WIDE, 4 * WIDE)
SIDE = slice(4 * WIDE, 4 * WIDE + GROUP)


def halves(x):
    high = x.astype(jnp.bfloat16)
    return high, (x - high.astype(jnp.float32)).astype(jnp.bfloat16)


def nt_dot(a, b):
    return lax.dot_general(a, b, (((1,), (1,)), ((), ())), preferred_element_type=jnp.float32)


def right_product(x, stacked):
    high, low = halves(x)
    return jnp.dot(
        jnp.concatenate([high, low, high], axis=1), stacked, preferred_element_type=jnp.float32
    )


def local_kernel(sources, kept, *refs):
    token_refs, upstream_refs = refs[:sources], refs[sources : 2 * sources]
    moment_ref, spot_ref, matrix_ref = refs[2 * sources : 2 * sources + 3]
    next_ref, message_ref, half_ref, scaled_ref, base_ref, value_ref = refs[-6:]
    rows, cols = moment_ref.shape
    per_row = LANES // kept
    lane = lax.broadcasted_iota(jnp.int32, (8, LANES), 1)
    first = lane < 2 * kept
    shift = GROUP * ((lane // kept) % 2)
    side = matrix_ref[SIDE, :].astype(jnp.float32)
    side = side[:, :LANES] + side[:, LANES:]
    table = [side[8 * k : 8 * k + 8, :] for k in range(GROUP // 8)]
    lane_group = lax.broadcasted_iota(jnp.int32, (WIDE, LANES), 1) // kept
    row_group = lax.broadcasted_iota(jnp.int32, (WIDE, LANES), 0) // GROUP
    lane_wide = lax.broadcasted_iota(jnp.int32, (GROUP, 2 * LANES), 1) % LANES // kept
    zero = jnp.zeros((), jnp.bfloat16)
    gradient = lax.dot_general(
        jnp.concatenate([r[...] for r in token_refs], axis=0),
        jnp.concatenate([r[...] for r in upstream_refs], axis=0),
        (((0,), (0,)), ((), ())),
        preferred_element_type=jnp.float32,
    )
    next_ref[...] = momentum_decay * moment_ref[...] + gradient
    for c in range(0, cols // WIDE, 2):
        spans = [slice(b * WIDE, b * WIDE + WIDE) for b in (c, c + 1)]
        both = jnp.concatenate([next_ref[:, span] for span in spans], axis=0)
        both = right_product(both, matrix_ref[FORWARD, :])
        half_ref[:, spans[0]] = both[:rows]
        half_ref[:, spans[1]] = both[rows:]
    for p in range(rows // GROUP):
        for c in range(cols // WIDE):
            at = p * (cols // WIDE) + c
            spots = jnp.broadcast_to(spot_ref[0, at : at + 1, :], (8, LANES))
            upper, lower = spots // GROUP, spots % GROUP
            where = lower + shift
            total = jnp.zeros((8, LANES), jnp.float32)
            starts = [p * GROUP + 8 * k for k in range(GROUP // 8)]
            low_span = slice(c * WIDE, c * WIDE + LANES)
            high_span = slice(c * WIDE + LANES, c * WIDE + WIDE)
            ones = [jnp.take_along_axis(half_ref[b : b + 8, low_span], where, axis=1) for b in starts]
            twos = [jnp.take_along_axis(half_ref[b : b + 8, high_span], where, axis=1) for b in starts]
            upper_rows = [jnp.take_along_axis(t, upper, axis=1) for t in table]
            lower_rows = [jnp.take_along_axis(t, lower, axis=1) for t in table]
            for one, two, up in zip(ones, twos, upper_rows):
                total = total + jnp.where(first, one, two) * up
            value = jnp.sum(total, axis=0, keepdims=True)
            value_ref[at : at + 1, :] = value
            s_high, s_low = halves(jnp.concatenate(upper_rows, axis=0) * value)
            b_high, b_low = halves(jnp.concatenate(lower_rows, axis=0))
            scaled_ref[at] = jnp.concatenate([s_high, s_low], axis=1)
            base_ref[at] = jnp.concatenate([b_high, b_low], axis=1)
    for p in range(rows // GROUP):
        for c in range(cols // WIDE):
            at = p * (cols // WIDE) + c
            scaled, base = scaled_ref[at], base_ref[at]
            b_high, b_low = base[:, :LANES], base[:, LANES:]
            b_high = jnp.concatenate([b_high, b_high], axis=1)
            b_low = jnp.concatenate([b_low, b_low], axis=1)
            masked = [jnp.where(lane_wide == a, scaled, zero) for a in range(per_row)]
            prod = nt_dot(
                jnp.concatenate(masked, axis=0),
                jnp.concatenate([b_high, b_high, b_low, b_low], axis=0),
            )
            prod = prod[:, :LANES] + prod[:, LANES:]
            left = lax.broadcasted_iota(jnp.int32, (GROUP, LANES), 1) < GROUP
            own = jnp.concatenate([jnp.where(left, prod[2 * b * GROUP : 2 * b * GROUP + GROUP], prod[2 * b * GROUP + GROUP : 2 * b * GROUP + 2 * GROUP]) for b in range(per_row // 2)], axis=1)
            block, span = slice(p * GROUP, p * GROUP + GROUP), slice(c * WIDE, c * WIDE + WIDE)
            next_ref[block, span] = next_ref[block, span] - own
    for n, part in enumerate(as_product(value_ref[...])):
        part = part.astype(jnp.bfloat16)
        for j in range(message_ref.shape[0]):
            message_ref[j, 0, n] = part


def as_product(value):
    best = value.astype(jnp.bfloat16).astype(jnp.float32)
    factor = jnp.ones_like(value)
    error = jnp.abs(best - value)
    for b in FACTORS:
        a = (value * (1.0 / b)).astype(jnp.bfloat16).astype(jnp.float32)
        trial = jnp.abs(a * b - value)
        better = trial < error
        error = jnp.where(better, trial, error)
        best = jnp.where(better, a, best)
        factor = jnp.where(better, b, factor)
    return best, factor


def shared_kernel(kept, *refs):
    message_ref, spot_ref, matrix_ref = refs[:3]
    step_ref, dense_ref = refs[-2:]
    replicas = message_ref.shape[0]
    depth = replicas * kept
    rows, cols = step_ref.shape
    per_row = LANES // kept
    level = lax.broadcasted_iota(jnp.int32, (GROUP, depth), 0)
    level = level.astype(jnp.float32).astype(jnp.bfloat16)
    zero = jnp.zeros((), jnp.bfloat16)

    def filled(x, at):
        tile = jnp.broadcast_to(x[at : at + 1], (16, depth)).astype(jnp.bfloat16)
        return jnp.concatenate([tile] * (GROUP // 16), axis=0)

    parts = [
        [message_ref[j, 0, n].astype(jnp.float32) for j in range(replicas)] for n in range(PARTS)
    ]
    parts.append([spot_ref[j, 0].astype(jnp.int32) for j in range(replicas)])
    for a in range(per_row):
        span = slice(a * kept, a * kept + kept)
        best, factor, place = [jnp.concatenate([x[:, span] for x in p], axis=1) for p in parts]
        upper = (place // GROUP).astype(jnp.float32)
        lower = (place % GROUP).astype(jnp.float32)
        for at in range(best.shape[0]):
            p, c = at // (cols // WIDE), at % (cols // WIDE)
            hot_upper = jnp.where(level == filled(upper, at), filled(factor, at), zero)
            hot_lower = jnp.where(level == filled(lower, at), filled(best, at), zero)
            place = slice(c * WIDE + a * GROUP, c * WIDE + a * GROUP + GROUP)
            dense_ref[p * GROUP : p * GROUP + GROUP, place] = nt_dot(hot_upper, hot_lower)
    pieces = []
    for c in range(cols // WIDE):
        parts = []
        for p in range(rows // GROUP):
            tile = dense_ref[p * GROUP : p * GROUP + GROUP, c * WIDE : c * WIDE + WIDE]
            high, low = halves(tile)
            stack = jnp.concatenate([high, low, high], axis=0)
            parts.append(jnp.dot(matrix_ref[SIDE, : 3 * GROUP], stack, preferred_element_type=jnp.float32))
        high, low = halves(jnp.concatenate(parts, axis=0))
        for b in range(WIDE // LANES):
            span = slice(b * LANES, b * LANES + LANES)
            pieces.append(jnp.concatenate([high[:, span], low[:, span]], axis=1))
    product = jnp.dot(
        jnp.concatenate(pieces, axis=0), matrix_ref[RIGHT, :], preferred_element_type=jnp.float32
    )
    for b in range(len(pieces)):
        part = product[b * rows : b * rows + rows]
        update = part[:, :LANES] + part[:, LANES:]
        step_ref[:, b * LANES : b * LANES + LANES] = jnp.tanh(sharpness * update)


def swap(x, axis, count, offset):
    return lax.ppermute(x, axis, [(i, i ^ offset) for i in range(count)])


def local_call(
    sources, kept, blocks, at, slot, columns, incoming, moment, spots, matrices, next_moment, message
):
    _, col_count = moment.shape
    tok = columns[0].shape[0]
    spot_rows = spots.shape[1]
    whole = pl.BlockSpec(memory_space=pltpu.VMEM)
    aliased, aliases = [], {}
    for position, array in enumerate((next_moment, message)):
        if not isinstance(array, jax.ShapeDtypeStruct):
            aliases[2 * sources + 3 + len(aliased)] = position
            aliased.append(array)
    rows = blocks * WIDE
    return pl.pallas_call(
        functools.partial(local_kernel, sources, kept),
        grid=(blocks,),
        in_specs=[pl.BlockSpec((tok, WIDE), lambda i: (0, i))] * sources
        + [whole] * sources
        + [
            pl.BlockSpec((WIDE, col_count), lambda i: (at + i, 0)),
            pl.BlockSpec((1, spot_rows, LANES), lambda i: (at + i, 0, 0)),
            whole,
        ]
        + [pl.BlockSpec(memory_space=pl.ANY)] * len(aliased),
        out_specs=[
            pl.BlockSpec((WIDE, col_count), lambda i: (at + i, 0)),
            pl.BlockSpec(
                (message.shape[0], 1) + message.shape[2:], lambda i: (0, slot + i, 0, 0, 0)
            ),
        ],
        out_shape=[jax.ShapeDtypeStruct(x.shape, x.dtype) for x in (next_moment, message)],
        input_output_aliases=aliases,
        scratch_shapes=[pltpu.VMEM((WIDE, col_count), jnp.float32)]
        + [pltpu.VMEM((spot_rows, GROUP, 2 * LANES), jnp.bfloat16)] * 2
        + [pltpu.VMEM((spot_rows, LANES), jnp.float32)],
        compiler_params=pltpu.CompilerParams(vmem_limit_bytes=48 * 2**20),
        cost_estimate=pl.CostEstimate(
            flops=12 * rows * col_count * WIDE, bytes_accessed=8 * rows * col_count, transcendentals=0
        ),
        name="local",
    )(*columns, *incoming, moment, spots, matrices, *aliased)


def shared_call(kept, blocks, at, shape, message, spots, matrices, previous):
    col_count = shape[1]
    whole = pl.BlockSpec(memory_space=pltpu.VMEM)
    aliased = [] if previous is None else [previous]
    rows = blocks * WIDE
    return pl.pallas_call(
        functools.partial(shared_kernel, kept),
        grid=(blocks,),
        in_specs=[
            pl.BlockSpec((message.shape[0], 1) + message.shape[2:], lambda i: (0, i, 0, 0, 0)),
            pl.BlockSpec((spots.shape[0], 1) + spots.shape[2:], lambda i: (0, at + i, 0, 0)),
            whole,
        ]
        + [pl.BlockSpec(memory_space=pl.ANY)] * len(aliased),
        out_specs=pl.BlockSpec((WIDE, col_count), lambda i: (at + i, 0)),
        out_shape=jax.ShapeDtypeStruct(shape, jnp.float32),
        input_output_aliases={3: 0} if aliased else {},
        scratch_shapes=[pltpu.VMEM((WIDE, col_count), jnp.float32)],
        compiler_params=pltpu.CompilerParams(vmem_limit_bytes=48 * 2**20),
        cost_estimate=pl.CostEstimate(
            flops=12 * rows * col_count * WIDE, bytes_accessed=4 * rows * col_count, transcendentals=0
        ),
        name="shared",
    )(message, spots, matrices, *aliased)


def chunk_sizes(steps):
    if steps < 4:
        return [1] * steps, [[k] for k in range(steps)]
    first = steps // 2
    return [first, steps - first], [[0], [1]]
    first = steps // 4
    second = (steps - first) // 2
    return [first, second, steps - first - second], [[0, 1], [2]]


def per_device(n_fsdp, n_rep, activations, cotangent, momentum, positions):
    tokens, upstream, moment = activations[0], cotangent[0], momentum[0]
    row_count, col_count = moment.shape
    kept = positions.shape[2]
    steps = row_count // WIDE
    sizes, travel = chunk_sizes(steps)
    starts = [sum(sizes[:k]) for k in range(len(sizes))]
    chunks = len(sizes)
    spot_rows = WIDE * col_count // (GROUP * GROUP) * kept // LANES
    me = lax.axis_index("fsdp")
    half = n_fsdp // 2

    def pieces_of(k, me):
        return [
            lax.dynamic_slice_in_dim(
                tokens, (me ^ offset) * row_count + starts[k] * WIDE, sizes[k] * WIDE, 1
            )
            for offset in range(n_fsdp)
        ]

    def exchange(pieces):
        out = [pieces[0]]
        for offset in range(1, n_fsdp):
            out.append(swap(pieces[offset], "fsdp", n_fsdp, offset))
        return out

    incoming = {0: upstream}
    offset = half
    while offset:
        for known in list(incoming):
            incoming[known ^ offset] = swap(incoming[known], "fsdp", n_fsdp, offset)
        offset //= 2
    pieces = pieces_of(0, me)
    me, positions, pieces = lax.optimization_barrier((me, positions, pieces))
    all_columns = [exchange(pieces)]
    for k in range(1, chunks):
        pieces = pieces_of(k, me)
        all_columns.append(exchange(pieces))
    spots = positions[0].reshape(steps, spot_rows, LANES)

    def settled(x):
        return jnp.where(me >= 0, x, jnp.zeros((), x.dtype))

    incoming = [settled(upstream)] + [incoming[i] for i in range(1, n_fsdp)]

    cosines = dct_table(GROUP)
    matrices = settled(all_matrices(cosines))

    copies = jnp.broadcast_to(spots.astype(jnp.int16)[None], (n_rep,) + spots.shape)
    all_spots = lax.all_to_all(copies, "rep", split_axis=0, concat_axis=0, tiled=True)
    next_moment = jax.ShapeDtypeStruct((row_count, col_count), jnp.float32)
    step, gathered = None, []
    for members in travel:
        blocks = sum(sizes[k] for k in members)
        message = jax.ShapeDtypeStruct((n_rep, blocks, PARTS, spot_rows, LANES), jnp.bfloat16)
        for k in members:
            next_moment, message = local_call(
                n_fsdp, kept, sizes[k], starts[k], starts[k] - starts[members[0]],
                all_columns[k], incoming, moment, spots, matrices, next_moment, message,
            )
        gathered.append(
            lax.all_to_all(message, "rep", split_axis=0, concat_axis=0, tiled=True)
        )
    for g, members in enumerate(travel):
        step = shared_call(
            kept, gathered[g].shape[1], starts[members[0]], moment.shape, gathered[g], all_spots,
            matrices, step,
        )
    return (next_moment[None], step)


def solution(mesh):
    spec = P("rep", "fsdp", None)
    return jax.shard_map(
        functools.partial(per_device, mesh.shape["fsdp"], mesh.shape["rep"]),
        mesh=mesh,
        in_specs=(spec, spec, spec, spec),
        out_specs=(spec, P("fsdp", None)),
        check_vma=False,
    )
```
